32 devices in a mesh: tok: 4 (over y, x), col: 8 (over z, core).
Axes of the slice: x: 2, y: 2, z: 4, core: 2. Of those that a mesh axis runs over, the one named last changes fastest.
Arguments:
- activations: bfloat16 [8192, 8192], P('tok', 'col'), may hold values from -60 to 60, as said below
- weight: bfloat16 [8192, 8192], P('tok', 'col'), may hold values from -6 to 6
- keep_mask: int32 [8192, 8192], P('tok', 'col'), may hold values from 0 to 1
Outputs:
- new_weight: bfloat16 [8192, 8192], P('tok', 'col')
The draws below stay inside these ranges and needn't reach their ends.
Inputs may be any that keep to these rules, and one draw needn't show every extreme that they name: activations of calibration tokens.
All inputs are finite; a program needn't handle non-finite values.
Results may differ from the reference program's by a relative error of at most 0.00115.
Values may be sent and summed in bfloat16 or wider, within the bound.
No kernel may reach another device: no remote copies, remote signals or barrier semaphores. Data moves between devices by JAX's collectives and lax.ppermute only.
A program may use at most 128 MiB of HBM per device.

```python
import math
import jax
import jax.numpy as jnp
from jax import lax

C = 8192
R = 8192
B = 1024
ITERS = 4
TOKENS = 8192
N_COL = 8


def draw_activations(key, part):
    keys = jax.random.split(jax.random.fold_in(key, 11), 4)
    scales = jnp.exp(jax.random.uniform(keys[0], (C,), jnp.float32, 0.0, math.log(10.0)))
    latent = jax.random.normal(keys[1], (TOKENS, 4), jnp.float32)
    loading = jax.random.normal(keys[2], (4, C), jnp.float32)
    noise = jax.random.normal(keys[3], (TOKENS, C), jnp.float32)
    share = 0.2
    values = scales[None, :] * (noise + share * jnp.dot(latent, loading))
    return jnp.clip(values, -60.0, 60.0).astype(jnp.bfloat16)


def with_ends(result, key, least, top_value):
    shape = result.shape
    place = [jax.random.randint(jax.random.fold_in(key, axis), (), 0, shape[axis]) for axis in range(len(shape))]
    result = result.at[tuple(place)].set(least)
    longest = shape.index(max(shape))
    place[longest] = (place[longest] + 1) % shape[longest]
    return result.at[tuple(place)].set(top_value)


def level_of(key, dims, cuts, least, largest):
    def one(dim, parts):
        draws = jax.random.uniform(jax.random.fold_in(jax.random.fold_in(key, 6), dim), (parts,), jnp.float32, least / len(cuts), largest / len(cuts))
        return jnp.repeat(jnp.exp(draws), dims[dim] // parts).reshape((-1,) + (1,) * (len(dims) - dim - 1))

    loudness = one(*cuts[0])
    for cut in cuts[1:]:
        loudness = loudness * one(*cut)
    return loudness


def normal_values(rng, extent, deviation, reach, pieces=(), held_as=jnp.bfloat16):
    level = level_of(rng, extent, pieces, -0.22, 0.18) if pieces else 1.0
    entries = jax.random.normal(rng, extent, jnp.float32) * deviation * level
    return jnp.minimum(jnp.maximum(entries, -reach), reach).astype(held_as)


def setup_inputs(seed: int = 0) -> dict:
    seeds = jax.random.split(jax.random.key(seed), 4)
    activations = draw_activations(jax.random.fold_in(seeds[3], 71), 0)
    weight = normal_values(seeds[1], (R, C), 1.0, 6.0, ((0, 4), (1, 8)))
    keep_mask = with_ends(jax.random.randint(seeds[2], (R, C), 0, 2), jax.random.fold_in(seeds[2], 1), 0, 1).astype(jnp.int32)
    return dict(activations=activations, weight=weight, keep_mask=keep_mask)


def reference(activations, weight, keep_mask):
    highest = lax.Precision.HIGHEST
    total_tokens = activations.shape[0]
    columns = weight.shape[1]
    col_width = columns // N_COL
    panel_width = B // N_COL
    slots = jnp.arange(B, dtype=jnp.int32)
    panel_ids = (slots // panel_width * col_width + slots % panel_width).astype(jnp.int32)
    widened = activations.astype(jnp.float32)
    selected = jnp.take(widened, panel_ids, axis=1)
    hessian_panel = jnp.dot(widened.T, selected, precision=highest) / total_tokens
    block = jnp.take(hessian_panel, panel_ids, axis=0)
    identity = jnp.eye(B, dtype=jnp.float32)
    damped = block + 0.01 * jnp.mean(jnp.diagonal(block)) * identity
    iterate = identity / jnp.sqrt(jnp.sum(damped * damped))
    for sweep in range(ITERS):
        product = jnp.dot(iterate, damped, precision=highest)
        iterate = 2.0 * iterate - jnp.dot(product, iterate, precision=highest)
    pruned = weight.astype(jnp.float32) * (1 - keep_mask).astype(jnp.float32)
    pruned_panel = jnp.take(pruned, panel_ids, axis=1)
    factor = jnp.dot(pruned_panel, iterate, precision=highest)
    correction = jnp.dot(factor, hessian_panel.T, precision=highest)
    kept = keep_mask.astype(jnp.float32)
    return (kept * (weight.astype(jnp.float32) - correction)).astype(jnp.bfloat16)
```

```python
import functools

import jax
import jax.numpy as jnp
from jax import lax
from jax.experimental import pallas as pl
from jax.experimental.pallas import tpu as pltpu
from jax.sharding import PartitionSpec as P

B = 1024
ITERS = 4
BF16 = jnp.bfloat16
F32 = jnp.float32
VMEM_LIMIT = 60 << 20


def shift_chip(x, n_col, step):
    return lax.ppermute(x, "col", [(i, (i + 2 * step) % n_col) for i in range(n_col)])


def swap_core(x, n_col):
    return lax.ppermute(x, "col", [(i, i ^ 1) for i in range(n_col)])


def swap_tok(x, n_tok, bit):
    return lax.ppermute(x, "tok", [(i, i ^ bit) for i in range(n_tok)])


def gather_chips(x, n_col):
    chips = n_col // 2
    steps = [1] + list(range(2, chips - 1)) + ([chips - 1] if chips > 2 else [])
    return [x] + [shift_chip(x, n_col, s) for s in steps[: chips - 1]]


def sum_tok(parts, n_tok):
    bits = [1 << k for k in range(n_tok.bit_length() - 1)]
    half = len(bits) // 2
    orders = (bits, bits[half:] + bits[:half])
    parts = list(parts)
    for k in range(len(bits)):
        got = [swap_tok(p, n_tok, order[k]) for p, order in zip(parts, orders)]
        parts = [(p.astype(F32) + g.astype(F32)).astype(BF16) for p, g in zip(parts, got)]
    return parts


def scatter_tok(parts, n_tok):
    index = lax.axis_index("tok")
    count = n_tok.bit_length() - 1
    bits = list(range(count))
    half = count // 2
    orders = (bits, bits[half:] + bits[:half])
    rows = parts[0].shape[0] // n_tok
    parts = [p.reshape((2,) * count + (rows, p.shape[1])) for p in parts]
    for k in range(count):
        sent, kept = [], []
        for p, order in zip(parts, orders):
            axis = count - 1 - order[k]
            mine = (index >> order[k]) & 1
            sent.append(lax.dynamic_slice_in_dim(p, 1 - mine, 1, axis))
            kept.append(lax.dynamic_slice_in_dim(p, mine, 1, axis))
        got = [swap_tok(s, n_tok, 1 << order[k]) for s, order in zip(sent, orders)]
        parts = [a + b for a, b in zip(kept, got)]
    return [p.reshape(rows, p.shape[-1]) for p in parts]


def gather_tok(x, n_tok):
    if n_tok != 4:
        items = [x]
        bit = 1
        while bit < n_tok:
            items = items + [swap_tok(v, n_tok, bit) for v in items]
            bit *= 2
        return items
    half = x.shape[0] // 2
    over_x, over_y = swap_tok(x, n_tok, 1), swap_tok(x, n_tok, 2)
    upper = swap_tok(over_x[:half], n_tok, 2)
    lower = swap_tok(over_y[half:], n_tok, 1)
    return [x, over_x, over_y, jnp.concatenate([upper, lower], axis=0)]


def inverse_kernel(own_ref, other_ref, v_hi_ref, v_lo_ref, scale_ref, q, v, qa, qb, vb):
    size = q.shape[0]
    half = size // 2
    tile = min(256, half)
    n_tiles = size // tile

    q[:half, :] = own_ref[...].astype(F32)
    q[half:, :half] = other_ref[:, half:].astype(F32)
    q[half:, half:] = other_ref[:, :half].astype(F32)

    def rows_of(i):
        return pl.ds(pl.multiple_of(i * tile, tile), tile)

    def eye(i):
        r = lax.broadcasted_iota(jnp.int32, (tile, size), 0) + i * tile
        return r == lax.broadcasted_iota(jnp.int32, (tile, size), 1)

    def measure(i, carry):
        squares, trace = carry
        x = q[rows_of(i), :]
        squares += jnp.sum(x * x)
        trace += jnp.sum(jnp.where(eye(i), x, 0.0))
        return squares, trace

    squares, trace = lax.fori_loop(0, n_tiles, measure, (F32(0.0), F32(0.0)))
    damping = 0.01 * trace / size
    total = squares + 2.0 * damping * trace + size * damping * damping
    scale = lax.rsqrt(jnp.full((8, 128), total, F32))
    scale_ref[...] = scale
    scale = scale[0:1, 0:1]

    def begin(i, carry):
        x = (q[rows_of(i), :] + jnp.where(eye(i), damping, 0.0)) * scale
        q[rows_of(i), :] = x
        v[rows_of(i), :] = x
        qa[rows_of(i), :] = x.astype(BF16)
        vb[rows_of(i), :] = x.astype(BF16)
        return carry

    lax.fori_loop(0, n_tiles, begin, 0)

    def first(i, carry):
        x = 2.0 * q[rows_of(i), :] - jnp.dot(qa[rows_of(i), :], qa[...], preferred_element_type=F32)
        q[rows_of(i), :] = x
        qb[rows_of(i), :] = x.astype(BF16)
        return carry

    lax.fori_loop(0, n_tiles, first, 0)
    old, new = qb, qa
    weight = 2.0
    for step in range(1, ITERS):
        last = step == ITERS - 1

        def sweep(i, carry, old=old, new=new, weight=weight, last=last):
            rows = rows_of(i)
            qs = q[rows, :]
            vs = 2.0 * v[rows, :] + weight * qs - jnp.dot(vb[rows, :], old[...], preferred_element_type=F32)
            if last:
                hi = vs.astype(BF16)
                v_hi_ref[rows, :] = hi
                v_lo_ref[rows, :] = (vs - hi.astype(F32)).astype(BF16)
            else:
                v[rows, :] = vs
                qn = 2.0 * qs - jnp.dot(old[rows, :], old[...], preferred_element_type=F32)
                q[rows, :] = qn
                new[rows, :] = qn.astype(BF16)
                vb[rows, :] = vs.astype(BF16)
            return carry

        lax.fori_loop(0, n_tiles, sweep, 0)
        old, new = new, old
        weight *= 2.0


def inverse(own, other):
    size = B
    return pl.pallas_call(
        inverse_kernel,
        out_shape=[
            jax.ShapeDtypeStruct((size, size), BF16),
            jax.ShapeDtypeStruct((size, size), BF16),
            jax.ShapeDtypeStruct((8, 128), F32),
        ],
        in_specs=[pl.BlockSpec(memory_space=pltpu.VMEM)] * 2,
        out_specs=[pl.BlockSpec(memory_space=pltpu.VMEM)] * 3,
        scratch_shapes=[
            pltpu.VMEM((size, size), F32),
            pltpu.VMEM((size, size), F32),
            pltpu.VMEM((size, size), BF16),
            pltpu.VMEM((size, size), BF16),
            pltpu.VMEM((size, size), BF16),
        ],
        compiler_params=pltpu.CompilerParams(vmem_limit_bytes=VMEM_LIMIT),
        cost_estimate=pl.CostEstimate(flops=12 * size**3, bytes_accessed=8 * size**2, transcendentals=0),
        name="inverse",
    )(own, other)


def rows_kernel(h_ref, v_hi_ref, v_lo_ref, scale_ref, out_ref):
    h = h_ref[...]
    hi = h.astype(BF16)
    lo = (h - hi.astype(F32)).astype(BF16)
    product = jnp.dot(hi, v_hi_ref[...], preferred_element_type=F32)
    product += jnp.dot(lo, v_hi_ref[...], preferred_element_type=F32)
    product += jnp.dot(hi, v_lo_ref[...], preferred_element_type=F32)
    out_ref[...] = (scale_ref[0:1, 0:1] * (2.0**ITERS * h - product)).astype(BF16)


def solve_rows(h, v_hi, v_lo, scale):
    return pl.pallas_call(
        rows_kernel,
        out_shape=jax.ShapeDtypeStruct(h.shape, BF16),
        in_specs=[pl.BlockSpec(memory_space=pltpu.VMEM)] * 4,
        out_specs=pl.BlockSpec(memory_space=pltpu.VMEM),
        compiler_params=pltpu.CompilerParams(vmem_limit_bytes=VMEM_LIMIT),
        cost_estimate=pl.CostEstimate(
            flops=6 * h.shape[0] * B * B, bytes_accessed=4 * B * B, transcendentals=0
        ),
        name="solve_rows",
    )(h, v_hi, v_lo, scale)


def update_kernel(index_ref, weight_ref, mask_ref, pruned_ref, *rest):
    *pieces, out_ref = rest
    width = out_ref.shape[1] // len(pieces)
    for m, piece in enumerate(pieces):
        if len(pieces) > 1:
            place = jnp.bitwise_xor(index_ref[0], m)
            columns = pl.ds(pl.multiple_of(place * width, width), width)
        else:
            columns = slice(None)
        fix = lax.dot_general(
            pruned_ref[...], piece[...], (((1,), (1,)), ((), ())), preferred_element_type=F32
        )
        kept = weight_ref[:, columns].astype(F32) - fix
        out_ref[:, columns] = (mask_ref[:, columns].astype(F32) * kept).astype(BF16)


def update(weight, mask, pruned, pieces):
    rows, columns = weight.shape
    tile = min(256, rows)
    index = lax.axis_index("tok").astype(jnp.int32)
    if pieces[0].shape[0] % 128:
        order = jnp.arange(len(pieces), dtype=jnp.int32) ^ index
        pieces = [jnp.take(jnp.stack(pieces), order, axis=0).reshape(columns, -1)]
    index = index.reshape(1)
    block = pl.BlockSpec((tile, columns), lambda i, *_: (i, 0))
    return pl.pallas_call(
        update_kernel,
        out_shape=jax.ShapeDtypeStruct((rows, columns), BF16),
        grid_spec=pltpu.PrefetchScalarGridSpec(
            num_scalar_prefetch=1,
            grid=(rows // tile,),
            in_specs=[block, block, pl.BlockSpec((tile, pruned.shape[1]), lambda i, *_: (i, 0))]
            + [pl.BlockSpec(memory_space=pltpu.VMEM)] * len(pieces),
            out_specs=block,
        ),
        compiler_params=pltpu.CompilerParams(vmem_limit_bytes=VMEM_LIMIT),
        cost_estimate=pl.CostEstimate(
            flops=2 * rows * columns * B, bytes_accessed=10 * rows * columns, transcendentals=0
        ),
        name="update",
    )(index, weight, mask, pruned, *pieces)


def per_device(activations, weight, keep_mask):
    n_col = lax.axis_size("col")
    n_tok = lax.axis_size("tok")
    panel_width = B // n_col

    mine = jnp.concatenate(gather_chips(activations[:, :panel_width], n_col), axis=1)
    theirs = swap_core(mine, n_col)
    contract = functools.partial(
        lax.dot_general, dimension_numbers=(((0,), (0,)), ((), ())), preferred_element_type=F32
    )
    block_parts = sum_tok([contract(mine, x).astype(BF16) for x in (mine, theirs)], n_tok)
    own_rows = jnp.concatenate(block_parts, axis=1)
    other_rows = swap_core(own_rows, n_col)
    v_hi, v_lo, scale = inverse(own_rows, other_rows)

    panel_parts = scatter_tok([contract(activations, x) for x in (mine, theirs)], n_tok)
    solved = solve_rows(jnp.concatenate(panel_parts, axis=1), v_hi, v_lo, scale)
    pieces = gather_tok(solved, n_tok)

    pruned = jnp.where(keep_mask[:, :panel_width] == 0, weight[:, :panel_width], jnp.zeros((), BF16))
    pruned_mine = jnp.concatenate(gather_chips(pruned, n_col), axis=1)
    pruned_panel = jnp.concatenate([pruned_mine, swap_core(pruned_mine, n_col)], axis=1)
    return update(weight, keep_mask, pruned_panel, pieces)


def solution(mesh):
    return jax.shard_map(
        per_device,
        mesh=mesh,
        in_specs=(P("tok", "col"), P("tok", "col"), P("tok", "col")),
        out_specs=P("tok", "col"),
        check_vma=False,
    )
```

```python
import functools

import jax
import jax.numpy as jnp
from jax import lax
from jax.experimental import pallas as pl
from jax.experimental.pallas import tpu as pltpu
from jax.sharding import PartitionSpec as P


B = 1024
ITERS = 4
BF16 = jnp.bfloat16
F32 = jnp.float32


def shift_chip(x, n_col, step):
    return lax.ppermute(x, "col", [(i, (i + 2 * step) % n_col) for i in range(n_col)])


def swap_core(x, n_col):
    return lax.ppermute(x, "col", [(i, i ^ 1) for i in range(n_col)])


def swap_tok(x, n_tok, bit):
    return lax.ppermute(x, "tok", [(i, i ^ bit) for i in range(n_tok)])


TRANSPOSED = (((0,), (0,)), ((), ()))


def after(x, *others):
    return lax.optimization_barrier((x, *others))[0]


def joined(xs):
    return xs[0] if len(xs) == 1 else jnp.concatenate(xs, axis=1)


def block_kernel(rows, *refs):
    *panels, out_ref = refs
    column = 0
    for shard in rows:
        left = panels[2 * shard][...].T
        width = left.shape[0]
        for before in range(shard + 1):
            right = jnp.concatenate([panels[2 * before][...], panels[2 * before + 1][...]], axis=1)
            product = jnp.dot(left, right, preferred_element_type=F32)
            out_ref[:, column : column + 2 * width] = product.astype(BF16)
            column += 2 * width


def block_rows(panels, rows):
    width = panels[0].shape[1]
    count = sum(shard + 1 for shard in rows)
    return pl.pallas_call(
        functools.partial(block_kernel, rows),
        out_shape=jax.ShapeDtypeStruct((width, 2 * width * count), BF16),
        in_specs=[pl.BlockSpec(memory_space=pltpu.VMEM)] * len(panels),
        out_specs=pl.BlockSpec(memory_space=pltpu.VMEM),
        compiler_params=pltpu.CompilerParams(vmem_limit_bytes=16 << 20),
        cost_estimate=pl.CostEstimate(
            flops=4 * width * width * count * panels[0].shape[0],
            bytes_accessed=2 * len(panels) * panels[0].size,
            transcendentals=0,
        ),
        name="block_rows",
    )(*panels)


def panel_kernel(runs, index_ref, *refs):
    *panels, activations_ref, sent_ref, kept_ref = refs
    left = joined([ref[...] for ref in panels]).T
    sent, kept = runs
    width = kept_ref.shape[1] // len(kept)
    for out_ref, run in ((sent_ref, sent), (kept_ref, kept)):
        for place, m in enumerate(run):
            start = pl.multiple_of(jnp.bitwise_xor(index_ref[0], m) * width, width)
            product = jnp.dot(left, activations_ref[:, pl.ds(start, width)], preferred_element_type=F32)
            out_ref[:, place * width : (place + 1) * width] = product


def panel_products(*arguments):
    *panels, activations, bits = arguments
    kept = [0]
    for bit in reversed(bits[1:]):
        kept = kept + [m | bit for m in kept]
    sent = [m | bits[0] for m in kept]
    columns = activations.shape[1]
    width = columns // (2 * len(kept))
    index = lax.axis_index("tok").astype(jnp.int32)
    if width % 128:
        product = lax.dot_general(
            joined(panels), activations, TRANSPOSED, preferred_element_type=F32
        )
        runs = product.reshape(-1, 2 * len(kept), width)
        return [
            jnp.take(runs, jnp.array(run, jnp.int32) ^ index, axis=1).reshape(len(product), -1)
            for run in (sent, kept)
        ]
    height = sum(panel.shape[1] for panel in panels)
    shape = jax.ShapeDtypeStruct((height, width * len(kept)), F32)
    return pl.pallas_call(
        functools.partial(panel_kernel, (sent, kept)),
        out_shape=[shape, shape],
        in_specs=[pl.BlockSpec(memory_space=pltpu.SMEM)]
        + [pl.BlockSpec(memory_space=pltpu.VMEM)] * (len(panels) + 1),
        out_specs=[pl.BlockSpec(memory_space=pltpu.VMEM)] * 2,
        compiler_params=pltpu.CompilerParams(vmem_limit_bytes=16 << 20),
        cost_estimate=pl.CostEstimate(
            flops=2 * panels[0].shape[0] * height * columns, bytes_accessed=2 * activations.size, transcendentals=0
        ),
        name="panel_products",
    )(index.reshape(1), *panels, activations)


def scatter_tok(sent, kept, n_tok, bits):
    addends = [kept, swap_tok(sent, n_tok, bits[0])]
    width = kept.shape[1]
    for bit in bits[1:]:
        width //= 2
        total = addends[0][:, width : 2 * width]
        for x in addends[1:]:
            total = total + x[:, width : 2 * width]
        addends.append(swap_tok(total, n_tok, bit))
    return addends


def add_rounded(x, y):
    return (x.astype(F32) + y.astype(F32)).astype(BF16)


def sum_tok(x, n_tok, bits):
    for bit in bits:
        x = add_rounded(x, swap_tok(x, n_tok, bit))
    return x


def gather_tok(x, n_tok):
    if n_tok != 4:
        items = [x]
        bit = 1
        while bit < n_tok:
            items = items + [swap_tok(v, n_tok, bit) for v in items]
            bit *= 2
        return items
    half = x.shape[0] // 2
    over_x, over_y = swap_tok(x, n_tok, 1), swap_tok(x, n_tok, 2)
    upper = swap_tok(over_x[:half], n_tok, 2)
    lower = swap_tok(over_y[half:], n_tok, 1)
    return [x, over_x, over_y, jnp.concatenate([upper, lower], axis=0)]


def inverse_kernel(width, count, *refs):
    own, other = refs[:count], refs[count : 2 * count]
    v_hi_ref, v_lo_ref, scale_ref, q, v, qa, qb, vb = refs[2 * count :]
    size = q.shape[0]
    tile = 256 if size % 256 == 0 else size

    triangle = ((shard, before) for shard in range(size) for before in range(shard + 1))
    for mine, theirs in zip(own, other):
        for part in range(mine.shape[1] // (2 * width)):
            x = mine[:, part * 2 * width : (part + 1) * 2 * width].astype(F32)
            y = theirs[:, part * 2 * width : (part + 1) * 2 * width].astype(F32)
            y = jnp.concatenate([y[:, width:], y[:, :width]], axis=1)
            shard, before = next(triangle)
            rows = slice(2 * width * shard, 2 * width * (shard + 1))
            columns = slice(2 * width * before, 2 * width * (before + 1))
            x = jnp.concatenate([x, y], axis=0)
            q[rows, columns] = x
            if before < shard:
                q[columns, rows] = x.T

    squares, trace = F32(0.0), F32(0.0)
    eye = lax.broadcasted_iota(jnp.int32, (tile, tile), 0) == lax.broadcasted_iota(jnp.int32, (tile, tile), 1)
    spans = [slice(i, i + tile) for i in range(0, size, tile)]
    for rows in spans:
        x = q[rows, :]
        squares += jnp.sum(x * x)
        trace += jnp.sum(jnp.where(eye, q[rows, rows], 0.0))
    damping = 0.01 * trace / size
    total = squares + 2.0 * damping * trace + size * damping * damping
    scale = lax.rsqrt(jnp.full((8, 128), total, F32))
    scale_ref[...] = scale
    scale = scale[0:1, 0:1]
    for rows in spans:
        q[rows, rows] += jnp.where(eye, damping, 0.0)
        x = q[rows, :] * scale
        q[rows, :] = x
        v[rows, :] = x
        qa[rows, :] = x.astype(BF16)
        vb[rows, :] = x.astype(BF16)

    def put(ref, rows, part):
        ref[rows, : rows.stop] = part
        if rows.start:
            ref[: rows.start, rows] = part[:, : rows.start].T

    for rows in spans:
        n = rows.stop
        x = 2.0 * q[rows, :n] - jnp.dot(qa[rows, :], qa[:, :n], preferred_element_type=F32)
        q[rows, :n] = x
        put(qb, rows, x.astype(BF16))
    old, new = qb, qa
    weight = 2.0
    for step in range(1, ITERS):
        last = step == ITERS - 1
        for rows in spans:
            n = rows.stop
            qs = q[rows, :n]
            vs = 2.0 * v[rows, :n] + weight * qs
            vs = vs - jnp.dot(vb[rows, :], old[:, :n], preferred_element_type=F32)
            v[rows, :n] = vs
            if last:
                hi = vs.astype(BF16)
                put(v_hi_ref, rows, hi)
                put(v_lo_ref, rows, (vs - hi.astype(F32)).astype(BF16))
            else:
                qn = 2.0 * qs - jnp.dot(old[rows, :], old[:, :n], preferred_element_type=F32)
                q[rows, :n] = qn
                put(new, rows, qn.astype(BF16))
        if not last:
            for rows in spans:
                put(vb, rows, v[rows, : rows.stop].astype(BF16))
        old, new = new, old
        weight *= 2.0


def inverse(own, other):
    width = own[0].shape[0]
    size = B
    return pl.pallas_call(
        functools.partial(inverse_kernel, width, len(own)),
        out_shape=[
            jax.ShapeDtypeStruct((size, size), BF16),
            jax.ShapeDtypeStruct((size, size), BF16),
            jax.ShapeDtypeStruct((8, 128), F32),
        ],
        in_specs=[pl.BlockSpec(memory_space=pltpu.VMEM)] * (2 * len(own)),
        out_specs=[pl.BlockSpec(memory_space=pltpu.VMEM)] * 3,
        scratch_shapes=[
            pltpu.VMEM((size, size), F32),
            pltpu.VMEM((size, size), F32),
            pltpu.VMEM((size, size), BF16),
            pltpu.VMEM((size, size), BF16),
            pltpu.VMEM((size, size), BF16),
        ],
        compiler_params=pltpu.CompilerParams(vmem_limit_bytes=32 << 20),
        cost_estimate=pl.CostEstimate(flops=12 * size**3, bytes_accessed=8 * size**2, transcendentals=0),
        name="inverse",
    )(*own, *other)


def rows_kernel(counts, *refs):
    *h_refs, v_hi_ref, v_lo_ref, scale_ref, out_ref = refs
    width = out_ref.shape[1]
    parts = []
    for count in counts:
        addends, h_refs = h_refs[:count], h_refs[count:]
        total = addends[0][:, :width]
        for ref in addends[1:]:
            total = total + ref[:, :width]
        parts.append(total)
    h = jnp.concatenate(parts, axis=0)
    hi = h.astype(BF16)
    lo = (h - hi.astype(F32)).astype(BF16)
    times = functools.partial(jnp.dot, preferred_element_type=F32)
    product = times(v_hi_ref[...], hi) + times(v_hi_ref[...], lo) + times(v_lo_ref[...], hi)
    out_ref[...] = (scale_ref[0:1, 0:1] * (2.0**ITERS * h - product)).astype(BF16)


def solve_rows(parts, v_hi, v_lo, scale):
    width = parts[0][-1].shape[1]
    flat = [x for part in parts for x in part]
    return pl.pallas_call(
        functools.partial(rows_kernel, tuple(len(part) for part in parts)),
        out_shape=jax.ShapeDtypeStruct((v_hi.shape[0], width), BF16),
        in_specs=[pl.BlockSpec(memory_space=pltpu.VMEM)] * (len(flat) + 3),
        out_specs=pl.BlockSpec(memory_space=pltpu.VMEM),
        compiler_params=pltpu.CompilerParams(vmem_limit_bytes=24 << 20),
        cost_estimate=pl.CostEstimate(flops=6 * width * B * B, bytes_accessed=4 * B * B, transcendentals=0),
        name="solve_rows",
    )(*flat, v_hi, v_lo, scale)


def pruned_kernel(weight_ref, mask_ref, out_ref):
    out_ref[...] = jnp.where(mask_ref[...] == 0, weight_ref[...], jnp.zeros((), BF16))


def pruned_columns(weight, mask, width):
    if width % 128:
        return jnp.where(mask[:, :width] == 0, weight[:, :width], jnp.zeros((), BF16))
    block = pl.BlockSpec((weight.shape[0], width), lambda i: (0, 0))
    return pl.pallas_call(
        pruned_kernel,
        out_shape=jax.ShapeDtypeStruct((weight.shape[0], width), BF16),
        grid=(1,),
        in_specs=[block, block],
        out_specs=block,
        compiler_params=pltpu.CompilerParams(vmem_limit_bytes=8 << 20),
        cost_estimate=pl.CostEstimate(flops=0, bytes_accessed=8 * weight.shape[0] * width, transcendentals=0),
        name="pruned_columns",
    )(weight, mask)


def update_kernel(index_ref, weight_ref, mask_ref, pruned_ref, *rest):
    *pieces, out_ref = rest
    width = out_ref.shape[1] // len(pieces)
    for m, piece in enumerate(pieces):
        if len(pieces) > 1:
            place = jnp.bitwise_xor(index_ref[0], m)
            columns = pl.ds(pl.multiple_of(place * width, width), width)
        else:
            columns = slice(None)
        fix = jnp.dot(pruned_ref[...], piece[...], preferred_element_type=F32)
        kept = weight_ref[:, columns].astype(F32) - fix
        out_ref[:, columns] = (mask_ref[:, columns].astype(F32) * kept).astype(BF16)


def update(weight, mask, pruned, pieces):
    rows, columns = weight.shape
    tile = min(512, rows)
    index = lax.axis_index("tok").astype(jnp.int32)
    if pieces[0].shape[1] % 128:
        order = jnp.arange(len(pieces), dtype=jnp.int32) ^ index
        pieces = jnp.take(jnp.stack(pieces), order, axis=0)
        pieces = [jnp.moveaxis(pieces, 0, 1).reshape(pieces.shape[1], columns)]
    index = index.reshape(1)
    block = pl.BlockSpec((tile, columns), lambda i, *_: (i, 0))
    return pl.pallas_call(
        update_kernel,
        out_shape=jax.ShapeDtypeStruct((rows, columns), BF16),
        grid_spec=pltpu.PrefetchScalarGridSpec(
            num_scalar_prefetch=1,
            grid=(rows // tile,),
            in_specs=[block, block, pl.BlockSpec((tile, pruned.shape[1]), lambda i, *_: (i, 0))]
            + [pl.BlockSpec(memory_space=pltpu.VMEM)] * len(pieces),
            out_specs=block,
        ),
        compiler_params=pltpu.CompilerParams(vmem_limit_bytes=32 << 20),
        cost_estimate=pl.CostEstimate(
            flops=2 * rows * columns * B, bytes_accessed=10 * rows * columns, transcendentals=0
        ),
        name="update",
    )(index, weight, mask, pruned, *pieces)


def gather_and_sum(activations, n_col, n_tok, bits, turned):
    chips = n_col // 2
    own = activations[:, : B // n_col]
    panels, sums, parts = [], [], []
    for k in range(chips):
        mine = own if k == 0 else shift_chip(own, n_col, k)
        panels += [mine, swap_core(mine, n_col)]
        order = turned if k % 2 else bits
        if k:
            rows = (0, 1) if k == 1 else (k,)
            sums.append(sum_tok(block_rows(panels, rows), n_tok, order))
        parts.append(scatter_tok(*panel_products(*panels[-2:], activations, order), n_tok, order))
    return sums, [swap_core(x, n_col) for x in sums], parts, mine


def gather_and_sum_4(activations, n_col, n_tok, bits, turned):
    x, y = bits
    own = activations[:, : B // n_col]

    def swapped(array):
        return swap_core(array, n_col)

    def over(array, bit):
        return swap_tok(array, n_tok, bit)

    def added(a, b):
        return add_rounded(a, b)

    def second_step(kept, arrived, bit):
        width = kept.shape[1] // 2
        total = kept[:, width:] + arrived[:, width:]
        return [kept, arrived, over(total, bit)]

    first = shift_chip(own, n_col, 1)
    second = shift_chip(first, n_col, 1)
    third = shift_chip(own, n_col, -1)
    panels = [own, swapped(own)]
    sent, kept = panel_products(*panels, activations, bits)
    part_0 = second_step(kept, over(sent, x), y)

    panels += [first, swapped(first)]
    rows_1 = block_rows(panels, (0, 1))
    total_1 = added(rows_1, over(rows_1, x))
    sum_1 = added(total_1, over(total_1, y))
    sent, kept = panel_products(panels[2], activations, bits)
    part_1 = second_step(kept, over(sent, x), y)
    sent, kept = panel_products(panels[3], activations, turned)
    part_2 = second_step(kept, over(sent, y), x)

    panels += [second, swapped(second), third, swapped(third)]
    rows_3 = block_rows(panels, (2, 3))
    middle = rows_3.shape[1] // 2
    left, right = rows_3[:, :middle], rows_3[:, middle:]
    left = added(left, over(left, x))
    right = added(right, over(right, y))
    sum_3 = [added(left, over(left, y)), added(right, over(right, x))]
    sum_3 = jnp.concatenate(sum_3, axis=1)
    sent, kept = panel_products(*panels[4:6], after(activations, rows_3), bits)
    part_3 = second_step(kept, over(sent, x), y)
    sent, kept = panel_products(*panels[6:], after(activations, rows_3), turned)
    part_4 = second_step(kept, over(sent, y), x)

    sums = [sum_1, sum_3]
    others = [swapped(v) for v in sums]
    return sums, others, [part_0, part_1, part_2, part_3, part_4], rows_3


def per_device(activations, weight, keep_mask):
    n_col = lax.axis_size("col")
    n_tok = lax.axis_size("tok")
    panel_width = B // n_col
    chips = n_col // 2
    bits = [1 << k for k in range(n_tok.bit_length() - 1)]
    turned = bits[len(bits) // 2 :] + bits[: len(bits) // 2]

    gather = gather_and_sum_4 if (chips, n_tok) == (4, 4) else gather_and_sum
    sums, others, parts, _ = gather(activations, n_col, n_tok, bits, turned)
    v_hi, v_lo, scale = inverse(sums, others)
    solved = solve_rows(parts, v_hi, v_lo, scale)
    pieces = gather_tok(solved, n_tok)

    pruned = pruned_columns(weight, keep_mask, panel_width)
    steps = [1, 2, -1] if chips == 4 else range(1, chips)
    pruned = [pruned] + [shift_chip(pruned, n_col, s) for s in steps]
    pruned_panel = jnp.concatenate([x for a in pruned for x in (a, swap_core(a, n_col))], axis=1)
    return update(weight, keep_mask, pruned_panel, pieces)


def solution(mesh):
    return jax.shard_map(
        per_device,
        mesh=mesh,
        in_specs=(P("tok", "col"), P("tok", "col"), P("tok", "col")),
        out_specs=P("tok", "col"),
        check_vma=False,
    )
```

```python
import functools

import jax
import jax.numpy as jnp
from jax import lax
from jax.experimental import pallas as pl
from jax.experimental.pallas import tpu as pltpu
from jax.sharding import PartitionSpec as P


B = 1024
ITERS = 4
BF16 = jnp.bfloat16
F32 = jnp.float32


def shift_chip(x, n_col, step):
    return lax.ppermute(x, "col", [(i, (i + 2 * step) % n_col) for i in range(n_col)])


def swap_core(x, n_col):
    return lax.ppermute(x, "col", [(i, i ^ 1) for i in range(n_col)])


def swap_tok(x, n_tok, bit):
    return lax.ppermute(x, "tok", [(i, i ^ bit) for i in range(n_tok)])


TRANSPOSED = (((0,), (0,)), ((), ()))


def after(x, *others):
    return lax.optimization_barrier((x, *others))[0]


def joined(xs):
    return xs[0] if len(xs) == 1 else jnp.concatenate(xs, axis=1)


def block_kernel(rows, *refs):
    *panels, out_ref = refs
    column = 0
    for shard in rows:
        left = panels[2 * shard][...].T
        width = left.shape[0]
        for before in range(shard + 1):
            right = jnp.concatenate([panels[2 * before][...], panels[2 * before + 1][...]], axis=1)
            product = jnp.dot(left, right, preferred_element_type=F32)
            out_ref[:, column : column + 2 * width] = product.astype(BF16)
            column += 2 * width


def block_rows(panels, rows):
    width = panels[0].shape[1]
    count = sum(shard + 1 for shard in rows)
    return pl.pallas_call(
        functools.partial(block_kernel, rows),
        out_shape=jax.ShapeDtypeStruct((width, 2 * width * count), BF16),
        in_specs=[pl.BlockSpec(memory_space=pltpu.VMEM)] * len(panels),
        out_specs=pl.BlockSpec(memory_space=pltpu.VMEM),
        compiler_params=pltpu.CompilerParams(vmem_limit_bytes=16 << 20),
        cost_estimate=pl.CostEstimate(
            flops=4 * width * width * count * panels[0].shape[0],
            bytes_accessed=2 * len(panels) * panels[0].size,
            transcendentals=0,
        ),
        name="block_rows",
    )(*panels)


def panel_kernel(runs, index_ref, *refs):
    outs = refs[-len(runs) :]
    *panels, activations_ref = refs[: -len(runs)]
    left = joined([ref[...] for ref in panels]).T
    width = outs[0].shape[1] // len(runs[0])
    for out_ref, run in zip(outs, runs):
        for place, m in enumerate(run):
            start = pl.multiple_of(jnp.bitwise_xor(index_ref[0], m) * width, width)
            product = jnp.dot(left, activations_ref[:, pl.ds(start, width)], preferred_element_type=F32)
            out_ref[:, place * width : (place + 1) * width] = product


def panel_products(panels, activations, runs):
    columns = activations.shape[1]
    width = columns // sum(len(run) for run in runs)
    index = lax.axis_index("tok").astype(jnp.int32)
    if width % 128:
        product = lax.dot_general(joined(panels), activations, TRANSPOSED, preferred_element_type=F32)
        pieces = product.reshape(product.shape[0], -1, width)
        return [
            jnp.take(pieces, jnp.array(run, jnp.int32) ^ index, axis=1).reshape(product.shape[0], -1)
            for run in runs
        ]
    height = sum(panel.shape[1] for panel in panels)
    return pl.pallas_call(
        functools.partial(panel_kernel, runs),
        out_shape=[jax.ShapeDtypeStruct((height, width * len(run)), F32) for run in runs],
        in_specs=[pl.BlockSpec(memory_space=pltpu.SMEM)]
        + [pl.BlockSpec(memory_space=pltpu.VMEM)] * (len(panels) + 1),
        out_specs=[pl.BlockSpec(memory_space=pltpu.VMEM)] * len(runs),
        compiler_params=pltpu.CompilerParams(vmem_limit_bytes=16 << 20),
        cost_estimate=pl.CostEstimate(
            flops=2 * panels[0].shape[0] * height * columns,
            bytes_accessed=2 * activations.size,
            transcendentals=0,
        ),
        name="panel_products",
    )(index.reshape(1), *panels, activations)


def halving(bits):
    kept = [0]
    for bit in reversed(bits[1:]):
        kept = kept + [m | bit for m in kept]
    return [m | bits[0] for m in kept], kept


def scatter_tok(sent, kept, n_tok, bits):
    addends = [kept, swap_tok(sent, n_tok, bits[0])]
    width = kept.shape[1]
    for bit in bits[1:]:
        width //= 2
        total = addends[0][:, width : 2 * width]
        for x in addends[1:]:
            total = total + x[:, width : 2 * width]
        addends.append(swap_tok(total, n_tok, bit))
    return addends


def add_rounded(x, y):
    return (x.astype(F32) + y.astype(F32)).astype(BF16)


def sum_tok(x, n_tok, bits):
    for bit in bits:
        x = add_rounded(x, swap_tok(x, n_tok, bit))
    return x


def gather_tok(x, n_tok):
    if n_tok != 4:
        items = [x]
        bit = 1
        while bit < n_tok:
            items = items + [swap_tok(v, n_tok, bit) for v in items]
            bit *= 2
        return items
    half = x.shape[0] // 2
    over_x, over_y = swap_tok(x, n_tok, 1), swap_tok(x, n_tok, 2)
    upper = swap_tok(over_x[:half], n_tok, 2)
    lower = swap_tok(over_y[half:], n_tok, 1)
    return [x, over_x, over_y, jnp.concatenate([upper, lower], axis=0)]


def inverse_kernel(width, count, *refs):
    own, other = refs[:count], refs[count : 2 * count]
    v_hi_ref, v_lo_ref, scale_ref, q, v, qa, qb, vb = refs[2 * count :]
    size = q.shape[0]
    tile = 256 if size % 256 == 0 else size

    triangle = ((shard, before) for shard in range(size) for before in range(shard + 1))
    for mine, theirs in zip(own, other):
        for part in range(mine.shape[1] // (2 * width)):
            x = mine[:, part * 2 * width : (part + 1) * 2 * width].astype(F32)
            y = theirs[:, part * 2 * width : (part + 1) * 2 * width].astype(F32)
            y = jnp.concatenate([y[:, width:], y[:, :width]], axis=1)
            shard, before = next(triangle)
            rows = slice(2 * width * shard, 2 * width * (shard + 1))
            columns = slice(2 * width * before, 2 * width * (before + 1))
            x = jnp.concatenate([x, y], axis=0)
            q[rows, columns] = x
            if before < shard:
                q[columns, rows] = x.T

    squares, trace = F32(0.0), F32(0.0)
    eye = lax.broadcasted_iota(jnp.int32, (tile, tile), 0) == lax.broadcasted_iota(jnp.int32, (tile, tile), 1)
    spans = [slice(i, i + tile) for i in range(0, size, tile)]
    for rows in spans:
        x = q[rows, :]
        squares += jnp.sum(x * x)
        trace += jnp.sum(jnp.where(eye, q[rows, rows], 0.0))
    damping = 0.01 * trace / size
    total = squares + 2.0 * damping * trace + size * damping * damping
    scale = lax.rsqrt(jnp.full((8, 128), total, F32))
    scale_ref[...] = scale
    scale = scale[0:1, 0:1]
    for rows in spans:
        q[rows, rows] += jnp.where(eye, damping, 0.0)
        x = q[rows, :] * scale
        q[rows, :] = x
        v[rows, :] = x
        qa[rows, :] = x.astype(BF16)
        vb[rows, :] = x.astype(BF16)

    def put(ref, rows, part):
        ref[rows, : rows.stop] = part
        if rows.start:
            ref[: rows.start, rows] = part[:, : rows.start].T

    for rows in spans:
        n = rows.stop
        x = 2.0 * q[rows, :n] - jnp.dot(qa[rows, :], qa[:, :n], preferred_element_type=F32)
        q[rows, :n] = x
        put(qb, rows, x.astype(BF16))
    old, new = qb, qa
    weight = 2.0
    for step in range(1, ITERS):
        last = step == ITERS - 1
        for rows in spans:
            n = rows.stop
            qs = q[rows, :n]
            vs = 2.0 * v[rows, :n] + weight * qs
            vs = vs - jnp.dot(vb[rows, :], old[:, :n], preferred_element_type=F32)
            v[rows, :n] = vs
            if last:
                hi = vs.astype(BF16)
                put(v_hi_ref, rows, hi)
                put(v_lo_ref, rows, (vs - hi.astype(F32)).astype(BF16))
            else:
                qn = 2.0 * qs - jnp.dot(old[rows, :], old[:, :n], preferred_element_type=F32)
                q[rows, :n] = qn
                put(new, rows, qn.astype(BF16))
        if not last:
            for rows in spans:
                put(vb, rows, v[rows, : rows.stop].astype(BF16))
        old, new = new, old
        weight *= 2.0


def inverse(own, other):
    width = own[0].shape[0]
    size = B
    return pl.pallas_call(
        functools.partial(inverse_kernel, width, len(own)),
        out_shape=[
            jax.ShapeDtypeStruct((size, size), BF16),
            jax.ShapeDtypeStruct((size, size), BF16),
            jax.ShapeDtypeStruct((8, 128), F32),
        ],
        in_specs=[pl.BlockSpec(memory_space=pltpu.VMEM)] * (2 * len(own)),
        out_specs=[pl.BlockSpec(memory_space=pltpu.VMEM)] * 3,
        scratch_shapes=[
            pltpu.VMEM((size, size), F32),
            pltpu.VMEM((size, size), F32),
            pltpu.VMEM((size, size), BF16),
            pltpu.VMEM((size, size), BF16),
            pltpu.VMEM((size, size), BF16),
        ],
        compiler_params=pltpu.CompilerParams(vmem_limit_bytes=24 << 20),
        cost_estimate=pl.CostEstimate(flops=12 * size**3, bytes_accessed=8 * size**2, transcendentals=0),
        name="inverse",
    )(*own, *other)


def rows_kernel(counts, *refs):
    *h_refs, v_hi_ref, v_lo_ref, scale_ref, out_ref = refs
    width = out_ref.shape[1]
    parts = []
    for count in counts:
        addends, h_refs = h_refs[:count], h_refs[count:]
        total = addends[0][:, :width]
        for ref in addends[1:]:
            total = total + ref[:, :width]
        parts.append(total)
    h = jnp.concatenate(parts, axis=0)
    hi = h.astype(BF16)
    lo = (h - hi.astype(F32)).astype(BF16)
    times = functools.partial(jnp.dot, preferred_element_type=F32)
    product = times(v_hi_ref[...], hi) + times(v_hi_ref[...], lo) + times(v_lo_ref[...], hi)
    out_ref[...] = (scale_ref[0:1, 0:1] * (2.0**ITERS * h - product)).astype(BF16)


def solve_rows(parts, v_hi, v_lo, scale):
    width = parts[0][-1].shape[1]
    flat = [x for part in parts for x in part]
    return pl.pallas_call(
        functools.partial(rows_kernel, tuple(len(part) for part in parts)),
        out_shape=jax.ShapeDtypeStruct((v_hi.shape[0], width), BF16),
        in_specs=[pl.BlockSpec(memory_space=pltpu.VMEM)] * (len(flat) + 3),
        out_specs=pl.BlockSpec(memory_space=pltpu.VMEM),
        compiler_params=pltpu.CompilerParams(vmem_limit_bytes=24 << 20),
        cost_estimate=pl.CostEstimate(flops=6 * width * B * B, bytes_accessed=4 * B * B, transcendentals=0),
        name="solve_rows",
    )(*flat, v_hi, v_lo, scale)


def pruned_kernel(weight_ref, mask_ref, pruned_ref, kept_ref):
    kept = mask_ref[...].astype(F32).astype(BF16)
    kept_ref[...] = kept
    width = weight_ref.shape[1]
    pruned_ref[...] = jnp.where(mask_ref[:, :width] == 0, weight_ref[...], jnp.zeros((), BF16))


def pruned_columns(weight, mask, width):
    if width % 128:
        return jnp.where(mask[:, :width] == 0, weight[:, :width], jnp.zeros((), BF16)), mask.astype(BF16)
    rows, columns = weight.shape
    tile = min(512, rows)
    narrow = pl.BlockSpec((tile, width), lambda i: (i, 0))
    wide = pl.BlockSpec((tile, columns), lambda i: (i, 0))
    return pl.pallas_call(
        pruned_kernel,
        out_shape=[
            jax.ShapeDtypeStruct((rows, width), BF16),
            jax.ShapeDtypeStruct((rows, columns), BF16),
        ],
        grid=(rows // tile,),
        in_specs=[narrow, wide],
        out_specs=[narrow, wide],
        compiler_params=pltpu.CompilerParams(vmem_limit_bytes=12 << 20),
        cost_estimate=pl.CostEstimate(flops=0, bytes_accessed=6 * weight.size, transcendentals=0),
        name="pruned_columns",
    )(weight, mask)


def update_kernel(runs, index_ref, weight_ref, mask_ref, pruned_ref, *rest):
    pieces = rest[: len(runs)]
    out_ref, stage, sems = rest[-3:]
    rows = weight_ref.shape[0]
    _, tile, width = stage.shape
    copies = []
    for i in range(0, rows, tile):
        for m, piece in zip(runs, pieces):
            slot = len(copies)
            place = (slice(i, i + tile), pl.ds(pl.multiple_of((index_ref[0] ^ m) * width, width), width))
            fix = jnp.dot(pruned_ref[i : i + tile, :], piece[...], preferred_element_type=F32)
            kept = weight_ref[place].astype(F32) - fix
            stage[slot] = (mask_ref[place].astype(F32) * kept).astype(BF16)
            copy = pltpu.make_async_copy(stage.at[slot], out_ref.at[place], sems.at[slot])
            copy.start()
            copies.append(copy)
    for copy in copies:
        copy.wait()


def update(weight, mask, pruned, pieces, runs, result=None):
    rows, columns = weight.shape
    width = pieces[0].shape[1]
    tile = min(512, rows)
    index = lax.axis_index("tok").astype(jnp.int32).reshape(1)
    extra = [] if result is None else [result]
    count = rows // tile * len(runs)
    return pl.pallas_call(
        functools.partial(update_kernel, runs),
        out_shape=jax.ShapeDtypeStruct((rows, columns), BF16),
        in_specs=[pl.BlockSpec(memory_space=pltpu.SMEM)]
        + [pl.BlockSpec(memory_space=pltpu.VMEM)] * (3 + len(pieces))
        + [pl.BlockSpec(memory_space=pl.ANY)] * len(extra),
        out_specs=pl.BlockSpec(memory_space=pl.ANY),
        scratch_shapes=[pltpu.VMEM((count, tile, width), BF16), pltpu.SemaphoreType.DMA((count,))],
        input_output_aliases={4 + len(pieces): 0} if extra else {},
        compiler_params=pltpu.CompilerParams(vmem_limit_bytes=20 << 20),
        cost_estimate=pl.CostEstimate(
            flops=2 * rows * width * len(runs) * B,
            bytes_accessed=6 * rows * width * len(runs),
            transcendentals=0,
        ),
        name="update",
    )(index, weight, mask, pruned, *pieces, *extra)


def updated(weight, mask, pruned, pieces):
    width = pieces[0].shape[1]
    if width % 128:
        order = jnp.arange(len(pieces), dtype=jnp.int32) ^ lax.axis_index("tok")
        whole = jnp.take(jnp.stack(pieces, axis=1), order, axis=1).reshape(B, -1)
        fix = jnp.dot(pruned, whole, preferred_element_type=F32)
        return (mask.astype(F32) * (weight.astype(F32) - fix)).astype(BF16)
    *most, last = pieces
    result = update(weight, mask, pruned, most, tuple(range(len(most))))
    return update(weight, mask, pruned, [last], (len(most),), result)


def gather_and_sum(activations, n_col, n_tok, bits, turned):
    chips = n_col // 2
    own = activations[:, : B // n_col]
    panels, sums, parts = [], [], []
    for k in range(chips):
        mine = own if k == 0 else shift_chip(own, n_col, k)
        panels += [mine, swap_core(mine, n_col)]
        order = turned if k % 2 else bits
        if k:
            rows = (0, 1) if k == 1 else (k,)
            sums.append(sum_tok(block_rows(panels, rows), n_tok, order))
        products = panel_products(panels[-2:], activations, halving(order))
        parts.append(scatter_tok(*products, n_tok, order))
    return sums, [swap_core(x, n_col) for x in sums], parts, mine


def gather_and_sum_4(activations, n_col, n_tok, bits, turned):
    x, y = bits
    own = activations[:, : B // n_col]

    def swapped(array):
        return swap_core(array, n_col)

    def over(array, bit):
        return swap_tok(array, n_tok, bit)

    def added(a, b):
        return add_rounded(a, b)

    def second_step(kept, arrived, bit):
        width = kept.shape[1] // 2
        total = kept[:, width:] + arrived[:, width:]
        return [kept, arrived, over(total, bit)]

    first = shift_chip(own, n_col, 1)
    second = shift_chip(first, n_col, 1)
    third = shift_chip(own, n_col, -1)
    panels = [own, swapped(own)]
    sent, kept = panel_products(panels[:1], activations, halving(bits))
    part_0 = second_step(kept, over(sent, x), y)
    sent, kept = panel_products(panels[1:], activations, halving(turned))
    part_0b = second_step(kept, over(sent, y), x)

    panels += [first, swapped(first)]
    rows_1 = block_rows(panels, (0, 1))
    total_1 = added(rows_1, over(rows_1, x))
    sum_1 = added(total_1, over(total_1, y))
    sent, kept = panel_products(panels[2:3], activations, halving(bits))
    part_1 = second_step(kept, over(sent, x), y)
    sent, kept = panel_products(panels[3:], activations, halving(turned))
    part_2 = second_step(kept, over(sent, y), x)

    panels += [second, swapped(second)]
    sent, kept = panel_products(panels[4:5], activations, halving(bits))
    part_3 = second_step(kept, over(sent, x), y)
    sent, kept = panel_products(panels[5:], activations, halving(turned))
    part_4 = second_step(kept, over(sent, y), x)

    panels += [third, swapped(third)]
    rows_3 = block_rows(panels, (2, 3))
    middle = rows_3.shape[1] // 2
    left, right = rows_3[:, :middle], rows_3[:, middle:]
    left = added(left, over(left, x))
    right = added(right, over(right, y))
    sum_3 = [added(left, over(left, y)), added(right, over(right, x))]
    sum_3 = jnp.concatenate(sum_3, axis=1)
    products = panel_products(panels[6:], after(activations, rows_3), ((0,), (1,), (2,), (3,)))
    part_5 = [products[0]] + [over(products[m], m) for m in (x, y, x | y)]

    sums = [sum_1, sum_3]
    others = [swapped(v) for v in sums]
    return sums, others, [part_0, part_0b, part_1, part_2, part_3, part_4, part_5], rows_3


def per_device(activations, weight, keep_mask):
    n_col = lax.axis_size("col")
    n_tok = lax.axis_size("tok")
    panel_width = B // n_col
    chips = n_col // 2
    bits = [1 << k for k in range(n_tok.bit_length() - 1)]
    turned = bits[len(bits) // 2 :] + bits[: len(bits) // 2]

    gather = gather_and_sum_4 if (chips, n_tok) == (4, 4) else gather_and_sum
    sums, others, parts, _ = gather(activations, n_col, n_tok, bits, turned)
    v_hi, v_lo, scale = inverse(sums, others)
    solved = solve_rows(parts, v_hi, v_lo, scale)
    pieces = gather_tok(solved, n_tok)

    pruned, mask = pruned_columns(weight, keep_mask, panel_width)
    if chips == 4:
        second = shift_chip(pruned, n_col, 1)
        third = shift_chip(second, n_col, 1)
        pruned = [pruned, second, third, shift_chip(pruned, n_col, -1)]
    else:
        pruned = [pruned] + [shift_chip(pruned, n_col, k) for k in range(1, chips)]
    pruned_panel = jnp.concatenate([x for a in pruned for x in (a, swap_core(a, n_col))], axis=1)
    return updated(weight, mask, pruned_panel, pieces)


def solution(mesh):
    return jax.shard_map(
        per_device,
        mesh=mesh,
        in_specs=(P("tok", "col"), P("tok", "col"), P("tok", "col")),
        out_specs=P("tok", "col"),
        check_vma=False,
    )
```

```python
import functools

import jax
import jax.numpy as jnp
from jax import lax
from jax.experimental import pallas as pl
from jax.experimental.pallas import tpu as pltpu
from jax.sharding import PartitionSpec as P


B = 1024
ITERS = 4
BF16 = jnp.bfloat16
F32 = jnp.float32


def shift_chip(x, n_col, step):
    return lax.ppermute(x, "col", [(i, (i + 2 * step) % n_col) for i in range(n_col)])


def swap_core(x, n_col):
    return lax.ppermute(x, "col", [(i, i ^ 1) for i in range(n_col)])


def swap_tok(x, n_tok, bit):
    return lax.ppermute(x, "tok", [(i, i ^ bit) for i in range(n_tok)])


TRANSPOSED = (((0,), (0,)), ((), ()))


def after(x, *others):
    return lax.optimization_barrier((x, *others))[0]


def joined(xs):
    return xs[0] if len(xs) == 1 else jnp.concatenate(xs, axis=1)


def block_kernel(rows, *refs):
    *panels, out_ref = refs
    column = 0
    for shard in rows:
        left = panels[2 * shard][...].T
        width = left.shape[0]
        for before in range(shard + 1):
            right = jnp.concatenate([panels[2 * before][...], panels[2 * before + 1][...]], axis=1)
            product = jnp.dot(left, right, preferred_element_type=F32)
            out_ref[:, column : column + 2 * width] = product.astype(BF16)
            column += 2 * width


def block_rows(panels, rows):
    width = panels[0].shape[1]
    count = sum(shard + 1 for shard in rows)
    return pl.pallas_call(
        functools.partial(block_kernel, rows),
        out_shape=jax.ShapeDtypeStruct((width, 2 * width * count), BF16),
        in_specs=[pl.BlockSpec(memory_space=pltpu.VMEM)] * len(panels),
        out_specs=pl.BlockSpec(memory_space=pltpu.VMEM),
        compiler_params=pltpu.CompilerParams(vmem_limit_bytes=16 << 20),
        cost_estimate=pl.CostEstimate(
            flops=4 * width * width * count * panels[0].shape[0],
            bytes_accessed=2 * len(panels) * panels[0].size,
            transcendentals=0,
        ),
        name="block_rows",
    )(*panels)


def panel_kernel(runs, index_ref, *refs):
    outs = refs[-len(runs) :]
    *panels, activations_ref = refs[: -len(runs)]
    left = joined([ref[...] for ref in panels]).T
    width = outs[0].shape[1] // len(runs[0])
    for out_ref, run in zip(outs, runs):
        for place, m in enumerate(run):
            start = pl.multiple_of(jnp.bitwise_xor(index_ref[0], m) * width, width)
            product = jnp.dot(left, activations_ref[:, pl.ds(start, width)], preferred_element_type=F32)
            out_ref[:, place * width : (place + 1) * width] = product


def panel_products(panels, activations, runs):
    columns = activations.shape[1]
    width = columns // sum(len(run) for run in runs)
    index = lax.axis_index("tok").astype(jnp.int32)
    if width % 128:
        product = lax.dot_general(joined(panels), activations, TRANSPOSED, preferred_element_type=F32)
        pieces = product.reshape(product.shape[0], -1, width)
        return [
            jnp.take(pieces, jnp.array(run, jnp.int32) ^ index, axis=1).reshape(product.shape[0], -1)
            for run in runs
        ]
    height = sum(panel.shape[1] for panel in panels)
    return pl.pallas_call(
        functools.partial(panel_kernel, runs),
        out_shape=[jax.ShapeDtypeStruct((height, width * len(run)), F32) for run in runs],
        in_specs=[pl.BlockSpec(memory_space=pltpu.SMEM)]
        + [pl.BlockSpec(memory_space=pltpu.VMEM)] * (len(panels) + 1),
        out_specs=[pl.BlockSpec(memory_space=pltpu.VMEM)] * len(runs),
        compiler_params=pltpu.CompilerParams(vmem_limit_bytes=16 << 20),
        cost_estimate=pl.CostEstimate(
            flops=2 * panels[0].shape[0] * height * columns,
            bytes_accessed=2 * activations.size,
            transcendentals=0,
        ),
        name="panel_products",
    )(index.reshape(1), *panels, activations)


def halving(bits):
    kept = [0]
    for bit in reversed(bits[1:]):
        kept = kept + [m | bit for m in kept]
    return [m | bits[0] for m in kept], kept


def scatter_tok(sent, kept, n_tok, bits):
    addends = [kept, swap_tok(sent, n_tok, bits[0])]
    width = kept.shape[1]
    for bit in bits[1:]:
        width //= 2
        total = addends[0][:, width : 2 * width]
        for x in addends[1:]:
            total = total + x[:, width : 2 * width]
        addends.append(swap_tok(total, n_tok, bit))
    return addends


def add_rounded(x, y):
    return (x.astype(F32) + y.astype(F32)).astype(BF16)


def sum_tok(x, n_tok, bits):
    for bit in bits:
        x = add_rounded(x, swap_tok(x, n_tok, bit))
    return x


def gather_tok(x, n_tok):
    if n_tok != 4:
        items = [x]
        bit = 1
        while bit < n_tok:
            items = items + [swap_tok(v, n_tok, bit) for v in items]
            bit *= 2
        return [[v] for v in items]
    half = x.shape[0] // 2
    upper, lower = x[:half], x[half:]
    over_x = [swap_tok(upper, n_tok, 1)]
    over_y = [swap_tok(lower, n_tok, 2)]
    over_x += [swap_tok(lower, n_tok, 1)]
    over_y = [swap_tok(upper, n_tok, 2)] + over_y
    both = [swap_tok(over_x[0], n_tok, 2), swap_tok(over_y[1], n_tok, 1)]
    return [[x], over_x, over_y, both]


def inverse_kernel(width, count, *refs):
    own, other = refs[:count], refs[count : 2 * count]
    v_hi_ref, v_lo_ref, scale_ref, q, v, qa, qb, vb = refs[2 * count :]
    size = q.shape[0]
    tile = 256 if size % 256 == 0 else size

    triangle = ((shard, before) for shard in range(size) for before in range(shard + 1))
    for mine, theirs in zip(own, other):
        for part in range(mine.shape[1] // (2 * width)):
            x = mine[:, part * 2 * width : (part + 1) * 2 * width].astype(F32)
            y = theirs[:, part * 2 * width : (part + 1) * 2 * width].astype(F32)
            y = jnp.concatenate([y[:, width:], y[:, :width]], axis=1)
            shard, before = next(triangle)
            rows = slice(2 * width * shard, 2 * width * (shard + 1))
            columns = slice(2 * width * before, 2 * width * (before + 1))
            x = jnp.concatenate([x, y], axis=0)
            q[rows, columns] = x
            if before < shard:
                q[columns, rows] = x.T

    squares, trace = F32(0.0), F32(0.0)
    eye = lax.broadcasted_iota(jnp.int32, (tile, tile), 0) == lax.broadcasted_iota(jnp.int32, (tile, tile), 1)
    spans = [slice(i, i + tile) for i in range(0, size, tile)]
    for rows in spans:
        x = q[rows, :]
        squares += jnp.sum(x * x)
        trace += jnp.sum(jnp.where(eye, q[rows, rows], 0.0))
    damping = 0.01 * trace / size
    total = squares + 2.0 * damping * trace + size * damping * damping
    scale = lax.rsqrt(jnp.full((8, 128), total, F32))
    scale_ref[...] = scale
    scale = scale[0:1, 0:1]
    for rows in spans:
        q[rows, rows] += jnp.where(eye, damping, 0.0)
        x = q[rows, :] * scale
        q[rows, :] = x
        v[rows, :] = x
        qa[rows, :] = x.astype(BF16)
        vb[rows, :] = x.astype(BF16)

    def put(ref, rows, part):
        ref[rows, : rows.stop] = part
        if rows.start:
            ref[: rows.start, rows] = part[:, : rows.start].T

    for rows in spans:
        n = rows.stop
        x = 2.0 * q[rows, :n] - jnp.dot(qa[rows, :], qa[:, :n], preferred_element_type=F32)
        q[rows, :n] = x
        put(qb, rows, x.astype(BF16))
    old, new = qb, qa
    weight = 2.0
    for step in range(1, ITERS):
        last = step == ITERS - 1
        for rows in spans:
            n = rows.stop
            qs = q[rows, :n]
            vs = 2.0 * v[rows, :n] + weight * qs
            vs = vs - jnp.dot(vb[rows, :], old[:, :n], preferred_element_type=F32)
            v[rows, :n] = vs
            if last:
                hi = vs.astype(BF16)
                put(v_hi_ref, rows, hi)
                put(v_lo_ref, rows, (vs - hi.astype(F32)).astype(BF16))
            else:
                qn = 2.0 * qs - jnp.dot(old[rows, :], old[:, :n], preferred_element_type=F32)
                q[rows, :n] = qn
                put(new, rows, qn.astype(BF16))
        if not last:
            for rows in spans:
                put(vb, rows, v[rows, : rows.stop].astype(BF16))
        old, new = new, old
        weight *= 2.0


def inverse(own, other):
    width = own[0].shape[0]
    size = B
    return pl.pallas_call(
        functools.partial(inverse_kernel, width, len(own)),
        out_shape=[
            jax.ShapeDtypeStruct((size, size), BF16),
            jax.ShapeDtypeStruct((size, size), BF16),
            jax.ShapeDtypeStruct((8, 128), F32),
        ],
        in_specs=[pl.BlockSpec(memory_space=pltpu.VMEM)] * (2 * len(own)),
        out_specs=[pl.BlockSpec(memory_space=pltpu.VMEM)] * 3,
        scratch_shapes=[
            pltpu.VMEM((size, size), F32),
            pltpu.VMEM((size, size), F32),
            pltpu.VMEM((size, size), BF16),
            pltpu.VMEM((size, size), BF16),
            pltpu.VMEM((size, size), BF16),
        ],
        compiler_params=pltpu.CompilerParams(vmem_limit_bytes=24 << 20),
        cost_estimate=pl.CostEstimate(flops=12 * size**3, bytes_accessed=8 * size**2, transcendentals=0),
        name="inverse",
    )(*own, *other)


def rows_kernel(counts, *refs):
    *h_refs, v_hi_ref, v_lo_ref, scale_ref, out_ref = refs
    width = out_ref.shape[1]
    parts = []
    for count in counts:
        addends, h_refs = h_refs[:count], h_refs[count:]
        total = addends[0][:, :width]
        for ref in addends[1:]:
            total = total + ref[:, :width]
        parts.append(total)
    h = jnp.concatenate(parts, axis=0)
    hi = h.astype(BF16)
    lo = (h - hi.astype(F32)).astype(BF16)
    times = functools.partial(jnp.dot, preferred_element_type=F32)
    product = times(v_hi_ref[...], hi) + times(v_hi_ref[...], lo) + times(v_lo_ref[...], hi)
    out_ref[...] = (scale_ref[0:1, 0:1] * (2.0**ITERS * h - product)).astype(BF16)


def solve_rows(parts, v_hi, v_lo, scale):
    width = parts[0][-1].shape[1]
    flat = [x for part in parts for x in part]
    return pl.pallas_call(
        functools.partial(rows_kernel, tuple(len(part) for part in parts)),
        out_shape=jax.ShapeDtypeStruct((v_hi.shape[0], width), BF16),
        in_specs=[pl.BlockSpec(memory_space=pltpu.VMEM)] * (len(flat) + 3),
        out_specs=pl.BlockSpec(memory_space=pltpu.VMEM),
        compiler_params=pltpu.CompilerParams(vmem_limit_bytes=24 << 20),
        cost_estimate=pl.CostEstimate(flops=6 * width * B * B, bytes_accessed=4 * B * B, transcendentals=0),
        name="solve_rows",
    )(*flat, v_hi, v_lo, scale)


def pruned_kernel(weight_ref, mask_ref, out_ref):
    out_ref[...] = jnp.where(mask_ref[...] == 0, weight_ref[...], jnp.zeros((), BF16))


def narrow_kernel(mask_ref, out_ref):
    out_ref[...] = mask_ref[...].astype(F32).astype(BF16)


def pruned_columns(weight, mask, width):
    if width % 128:
        return jnp.where(mask[:, :width] == 0, weight[:, :width], jnp.zeros((), BF16))
    block = pl.BlockSpec((weight.shape[0], width), lambda i: (0, 0))
    return pl.pallas_call(
        pruned_kernel,
        out_shape=jax.ShapeDtypeStruct((weight.shape[0], width), BF16),
        grid=(1,),
        in_specs=[block, block],
        out_specs=block,
        compiler_params=pltpu.CompilerParams(vmem_limit_bytes=8 << 20),
        cost_estimate=pl.CostEstimate(flops=0, bytes_accessed=8 * weight.shape[0] * width, transcendentals=0),
        name="pruned_columns",
    )(weight, mask)


def narrowed(mask):
    rows, columns = mask.shape
    block = pl.BlockSpec((min(512, rows), columns), lambda i: (i, 0))
    return pl.pallas_call(
        narrow_kernel,
        out_shape=jax.ShapeDtypeStruct(mask.shape, BF16),
        grid=(rows // min(512, rows),),
        in_specs=[block],
        out_specs=block,
        compiler_params=pltpu.CompilerParams(vmem_limit_bytes=12 << 20),
        cost_estimate=pl.CostEstimate(flops=0, bytes_accessed=6 * mask.size, transcendentals=0),
        name="narrowed",
    )(mask)


def update_kernel(runs, counts, index_ref, weight_ref, mask_ref, pruned_ref, *rest):
    out_ref, stage, sems = rest[-3:]
    pieces = []
    for count in counts:
        pieces.append(rest[:count])
        rest = rest[count:]
    rows = weight_ref.shape[0]
    _, tile, width = stage.shape
    copies = []
    for i in range(0, rows, tile):
        for m, piece in zip(runs, pieces):
            slot = len(copies)
            place = (slice(i, i + tile), pl.ds(pl.multiple_of((index_ref[0] ^ m) * width, width), width))
            fix, start = 0.0, 0
            for part in piece:
                left = pruned_ref[i : i + tile, start : start + part.shape[0]]
                fix += jnp.dot(left, part[...], preferred_element_type=F32)
                start += part.shape[0]
            kept = weight_ref[place].astype(F32) - fix
            stage[slot] = (mask_ref[place].astype(F32) * kept).astype(BF16)
            copy = pltpu.make_async_copy(stage.at[slot], out_ref.at[place], sems.at[slot])
            copy.start()
            copies.append(copy)
    for copy in copies:
        copy.wait()


def update(weight, mask, pruned, pieces, runs, result=None):
    rows, columns = weight.shape
    width = pieces[0][0].shape[1]
    counts = tuple(len(piece) for piece in pieces)
    pieces = [part for piece in pieces for part in piece]
    tile = min(512, rows)
    index = lax.axis_index("tok").astype(jnp.int32).reshape(1)
    extra = [] if result is None else [result]
    count = rows // tile * len(runs)
    return pl.pallas_call(
        functools.partial(update_kernel, runs, counts),
        out_shape=jax.ShapeDtypeStruct((rows, columns), BF16),
        in_specs=[pl.BlockSpec(memory_space=pltpu.SMEM)]
        + [pl.BlockSpec(memory_space=pltpu.VMEM)] * (3 + len(pieces))
        + [pl.BlockSpec(memory_space=pl.ANY)] * len(extra),
        out_specs=pl.BlockSpec(memory_space=pl.ANY),
        scratch_shapes=[pltpu.VMEM((count, tile, width), BF16), pltpu.SemaphoreType.DMA((count,))],
        input_output_aliases={4 + len(pieces): 0} if extra else {},
        compiler_params=pltpu.CompilerParams(vmem_limit_bytes=20 << 20),
        cost_estimate=pl.CostEstimate(
            flops=2 * rows * width * len(runs) * B,
            bytes_accessed=6 * rows * width * len(runs),
            transcendentals=0,
        ),
        name="update",
    )(index, weight, mask, pruned, *pieces, *extra)


def updated(weight, mask, pruned, pieces):
    width = pieces[0][0].shape[1]
    if width % 128:
        order = jnp.arange(len(pieces), dtype=jnp.int32) ^ lax.axis_index("tok")
        whole = [jnp.concatenate(piece, axis=0) for piece in pieces]
        whole = jnp.take(jnp.stack(whole, axis=1), order, axis=1).reshape(B, -1)
        fix = jnp.dot(pruned, whole, preferred_element_type=F32)
        return (mask.astype(F32) * (weight.astype(F32) - fix)).astype(BF16)
    *most, last = pieces
    result = update(weight, mask, pruned, most, tuple(range(len(most))))
    return update(weight, mask, pruned, [last], (len(most),), result)


def gather_and_sum(activations, n_col, n_tok, bits, turned):
    chips = n_col // 2
    own = activations[:, : B // n_col]
    panels, sums, parts = [], [], []
    for k in range(chips):
        mine = own if k == 0 else shift_chip(own, n_col, k)
        panels += [mine, swap_core(mine, n_col)]
        order = turned if k % 2 else bits
        if k:
            rows = (0, 1) if k == 1 else (k,)
            sums.append(sum_tok(block_rows(panels, rows), n_tok, order))
        products = panel_products(panels[-2:], activations, halving(order))
        parts.append(scatter_tok(*products, n_tok, order))
    return sums, [swap_core(x, n_col) for x in sums], parts, mine


def gather_and_sum_4(activations, n_col, n_tok, bits, turned):
    x, y = bits
    own = activations[:, : B // n_col]

    def swapped(array):
        return swap_core(array, n_col)

    def over(array, bit):
        return swap_tok(array, n_tok, bit)

    def added(a, b):
        return add_rounded(a, b)

    def second_step(kept, arrived, bit):
        width = kept.shape[1] // 2
        total = kept[:, width:] + arrived[:, width:]
        return [kept, arrived, over(total, bit)]

    first = shift_chip(own, n_col, 1)
    second = shift_chip(own, n_col, -1)
    third = shift_chip(first, n_col, 1)
    panels = [own, swapped(own)]
    sent, kept = panel_products(panels[:1], activations, halving(bits))
    part_0 = second_step(kept, over(sent, x), y)
    sent, kept = panel_products(panels[1:], activations, halving(turned))
    part_0b = second_step(kept, over(sent, y), x)

    panels += [first, swapped(first)]
    rows_1 = block_rows(panels, (0, 1))
    total_1 = added(rows_1, over(rows_1, x))
    sum_1 = added(total_1, over(total_1, y))
    sent, kept = panel_products(panels[2:3], activations, halving(bits))
    part_1 = second_step(kept, over(sent, x), y)
    sent, kept = panel_products(panels[3:], activations, halving(turned))
    part_2 = second_step(kept, over(sent, y), x)

    panels += [second, swapped(second)]
    sent, kept = panel_products(panels[4:5], activations, halving(bits))
    part_3 = second_step(kept, over(sent, x), y)
    sent, kept = panel_products(panels[5:], activations, halving(turned))
    part_4 = second_step(kept, over(sent, y), x)

    panels += [third, swapped(third)]
    rows_3 = block_rows(panels, (2, 3))
    middle = rows_3.shape[1] // 2
    left, right = rows_3[:, :middle], rows_3[:, middle:]
    left = added(left, over(left, x))
    right = added(right, over(right, y))
    sum_3 = [added(left, over(left, y)), added(right, over(right, x))]
    sum_3 = jnp.concatenate(sum_3, axis=1)
    products = panel_products(panels[6:], after(activations, rows_3), ((0,), (1,), (2,), (3,)))
    part_5 = [products[0]] + [over(products[m], m) for m in (x, y, x | y)]

    sums = [sum_1, sum_3]
    others = [swapped(v) for v in sums]
    return sums, others, [part_0, part_0b, part_1, part_2, part_3, part_4, part_5], rows_3


def per_device(activations, weight, keep_mask):
    n_col = lax.axis_size("col")
    n_tok = lax.axis_size("tok")
    panel_width = B // n_col
    chips = n_col // 2
    bits = [1 << k for k in range(n_tok.bit_length() - 1)]
    turned = bits[len(bits) // 2 :] + bits[: len(bits) // 2]

    gather = gather_and_sum_4 if (chips, n_tok) == (4, 4) else gather_and_sum
    sums, others, parts, _ = gather(activations, n_col, n_tok, bits, turned)
    v_hi, v_lo, scale = inverse(sums, others)
    solved = solve_rows(parts, v_hi, v_lo, scale)
    pieces = gather_tok(solved, n_tok)

    pruned = pruned_columns(weight, keep_mask, panel_width)
    mask = narrowed(keep_mask)
    if chips == 4:
        second = shift_chip(pruned, n_col, 1)
        third = shift_chip(second, n_col, 1)
        pruned = [pruned, second, shift_chip(pruned, n_col, -1), third]
    else:
        pruned = [pruned] + [shift_chip(pruned, n_col, k) for k in range(1, chips)]
    others = [swap_core(v, n_col) for v in pruned]
    pruned_panel = jnp.concatenate([x for pair in zip(pruned, others) for x in pair], axis=1)
    return updated(weight, mask, pruned_panel, pieces)


def solution(mesh):
    return jax.shard_map(
        per_device,
        mesh=mesh,
        in_specs=(P("tok", "col"), P("tok", "col"), P("tok", "col")),
        out_specs=P("tok", "col"),
        check_vma=False,
    )
```

```python
import functools

import jax
import jax.numpy as jnp
from jax import lax
from jax.experimental import pallas as pl
from jax.experimental.pallas import tpu as pltpu
from jax.sharding import PartitionSpec as P


B = 1024
ITERS = 4
BF16 = jnp.bfloat16
F32 = jnp.float32


def shift_chip(x, n_col, step):
    return lax.ppermute(x, "col", [(i, (i + 2 * step) % n_col) for i in range(n_col)])


def swap_core(x, n_col):
    return lax.ppermute(x, "col", [(i, i ^ 1) for i in range(n_col)])


def swap_tok(x, n_tok, bit):
    return lax.ppermute(x, "tok", [(i, i ^ bit) for i in range(n_tok)])


TRANSPOSED = (((0,), (0,)), ((), ()))


def joined(xs):
    return xs[0] if len(xs) == 1 else jnp.concatenate(xs, axis=1)


def block_kernel(rows, *refs):
    *panels, out_ref = refs
    column = 0
    for shard in rows:
        left = panels[2 * shard][...].T
        width = left.shape[0]
        for before in range(shard + 1):
            right = jnp.concatenate([panels[2 * before][...], panels[2 * before + 1][...]], axis=1)
            product = jnp.dot(left, right, preferred_element_type=F32)
            out_ref[:, column : column + 2 * width] = product.astype(BF16)
            column += 2 * width


def block_rows(panels, rows):
    width = panels[0].shape[1]
    count = sum(shard + 1 for shard in rows)
    return pl.pallas_call(
        functools.partial(block_kernel, rows),
        out_shape=jax.ShapeDtypeStruct((width, 2 * width * count), BF16),
        in_specs=[pl.BlockSpec(memory_space=pltpu.VMEM)] * len(panels),
        out_specs=pl.BlockSpec(memory_space=pltpu.VMEM),
        compiler_params=pltpu.CompilerParams(vmem_limit_bytes=16 << 20),
        cost_estimate=pl.CostEstimate(
            flops=4 * width * width * count * panels[0].shape[0],
            bytes_accessed=2 * len(panels) * panels[0].size,
            transcendentals=0,
        ),
        name="block_rows",
    )(*panels)


def panel_kernel(runs, index_ref, *refs):
    outs = refs[-len(runs) :]
    *panels, activations_ref = refs[: -len(runs)]
    left = joined([ref[...] for ref in panels]).T
    width = outs[0].shape[1] // len(runs[0])
    for out_ref, run in zip(outs, runs):
        for place, m in enumerate(run):
            start = pl.multiple_of(jnp.bitwise_xor(index_ref[0], m) * width, width)
            product = jnp.dot(left, activations_ref[:, pl.ds(start, width)], preferred_element_type=F32)
            out_ref[:, place * width : (place + 1) * width] = product


def panel_products(panels, activations, runs):
    columns = activations.shape[1]
    width = columns // sum(len(run) for run in runs)
    index = lax.axis_index("tok").astype(jnp.int32)
    if width % 128:
        product = lax.dot_general(joined(panels), activations, TRANSPOSED, preferred_element_type=F32)
        pieces = product.reshape(product.shape[0], -1, width)
        return [
            jnp.take(pieces, jnp.array(run, jnp.int32) ^ index, axis=1).reshape(product.shape[0], -1)
            for run in runs
        ]
    height = sum(panel.shape[1] for panel in panels)
    return pl.pallas_call(
        functools.partial(panel_kernel, runs),
        out_shape=[jax.ShapeDtypeStruct((height, width * len(run)), F32) for run in runs],
        in_specs=[pl.BlockSpec(memory_space=pltpu.SMEM)]
        + [pl.BlockSpec(memory_space=pltpu.VMEM)] * (len(panels) + 1),
        out_specs=[pl.BlockSpec(memory_space=pltpu.VMEM)] * len(runs),
        compiler_params=pltpu.CompilerParams(vmem_limit_bytes=16 << 20),
        cost_estimate=pl.CostEstimate(
            flops=2 * panels[0].shape[0] * height * columns,
            bytes_accessed=2 * activations.size,
            transcendentals=0,
        ),
        name="panel_products",
    )(index.reshape(1), *panels, activations)


def halving(bits):
    kept = [0]
    for bit in reversed(bits[1:]):
        kept = kept + [m | bit for m in kept]
    return [m | bits[0] for m in kept], kept


def scatter_tok(sent, kept, n_tok, bits):
    addends = [kept, swap_tok(sent, n_tok, bits[0])]
    width = kept.shape[1]
    for bit in bits[1:]:
        width //= 2
        total = addends[0][:, width : 2 * width]
        for x in addends[1:]:
            total = total + x[:, width : 2 * width]
        addends.append(swap_tok(total, n_tok, bit))
    return addends


def add_rounded(x, y):
    return (x.astype(F32) + y.astype(F32)).astype(BF16)


def sum_tok(x, n_tok, bits):
    for bit in bits:
        x = add_rounded(x, swap_tok(x, n_tok, bit))
    return x


def gather_tok(x, n_tok):
    if n_tok != 4:
        items = [x]
        bit = 1
        while bit < n_tok:
            items = items + [swap_tok(v, n_tok, bit) for v in items]
            bit *= 2
        return [[v] for v in items]
    half = x.shape[0] // 2
    upper, lower = x[:half], x[half:]
    over_x = [swap_tok(upper, n_tok, 1)]
    over_y = [swap_tok(lower, n_tok, 2)]
    over_x += [swap_tok(lower, n_tok, 1)]
    over_y = [swap_tok(upper, n_tok, 2)] + over_y
    both = [swap_tok(over_x[0], n_tok, 2), swap_tok(over_y[1], n_tok, 1)]
    return [[x], over_x, over_y, both]


def inverse_kernel(width, count, *refs):
    own, other = refs[:count], refs[count : 2 * count]
    v_hi_ref, v_lo_ref, scale_ref, q, v, qa, qb, vb = refs[2 * count :]
    size = q.shape[0]
    tile = 256 if size % 256 == 0 else size

    triangle = ((shard, before) for shard in range(size) for before in range(shard + 1))
    for mine, theirs in zip(own, other):
        for part in range(mine.shape[1] // (2 * width)):
            x = mine[:, part * 2 * width : (part + 1) * 2 * width].astype(F32)
            y = theirs[:, part * 2 * width : (part + 1) * 2 * width].astype(F32)
            y = jnp.concatenate([y[:, width:], y[:, :width]], axis=1)
            shard, before = next(triangle)
            rows = slice(2 * width * shard, 2 * width * (shard + 1))
            columns = slice(2 * width * before, 2 * width * (before + 1))
            x = jnp.concatenate([x, y], axis=0)
            q[rows, columns] = x
            if before < shard:
                q[columns, rows] = x.T

    squares, trace = F32(0.0), F32(0.0)
    eye = lax.broadcasted_iota(jnp.int32, (tile, tile), 0) == lax.broadcasted_iota(jnp.int32, (tile, tile), 1)
    spans = [slice(i, i + tile) for i in range(0, size, tile)]
    for rows in spans:
        x = q[rows, :]
        squares += jnp.sum(x * x)
        trace += jnp.sum(jnp.where(eye, q[rows, rows], 0.0))
    damping = 0.01 * trace / size
    total = squares + 2.0 * damping * trace + size * damping * damping
    scale = lax.rsqrt(jnp.full((8, 128), total, F32))
    scale_ref[...] = scale
    scale = scale[0:1, 0:1]
    for rows in spans:
        q[rows, rows] += jnp.where(eye, damping, 0.0)
        x = q[rows, :] * scale
        q[rows, :] = x
        v[rows, :] = x
        qa[rows, :] = x.astype(BF16)
        vb[rows, :] = x.astype(BF16)

    def put(ref, rows, part):
        ref[rows, : rows.stop] = part
        if rows.start:
            ref[: rows.start, rows] = part[:, : rows.start].T

    for rows in spans:
        n = rows.stop
        x = 2.0 * q[rows, :n] - jnp.dot(qa[rows, :], qa[:, :n], preferred_element_type=F32)
        q[rows, :n] = x
        put(qb, rows, x.astype(BF16))
    old, new = qb, qa
    weight = 2.0
    for step in range(1, ITERS):
        last = step == ITERS - 1
        for rows in spans:
            n = rows.stop
            qs = q[rows, :n]
            vs = 2.0 * v[rows, :n] + weight * qs
            vs = vs - jnp.dot(vb[rows, :], old[:, :n], preferred_element_type=F32)
            v[rows, :n] = vs
            if last:
                hi = vs.astype(BF16)
                put(v_hi_ref, rows, hi)
                put(v_lo_ref, rows, (vs - hi.astype(F32)).astype(BF16))
            else:
                qn = 2.0 * qs - jnp.dot(old[rows, :], old[:, :n], preferred_element_type=F32)
                q[rows, :n] = qn
                put(new, rows, qn.astype(BF16))
        if not last:
            for rows in spans:
                put(vb, rows, v[rows, : rows.stop].astype(BF16))
        old, new = new, old
        weight *= 2.0


def inverse(own, other):
    width = own[0].shape[0]
    size = B
    return pl.pallas_call(
        functools.partial(inverse_kernel, width, len(own)),
        out_shape=[
            jax.ShapeDtypeStruct((size, size), BF16),
            jax.ShapeDtypeStruct((size, size), BF16),
            jax.ShapeDtypeStruct((8, 128), F32),
        ],
        in_specs=[pl.BlockSpec(memory_space=pltpu.VMEM)] * (2 * len(own)),
        out_specs=[pl.BlockSpec(memory_space=pltpu.VMEM)] * 3,
        scratch_shapes=[
            pltpu.VMEM((size, size), F32),
            pltpu.VMEM((size, size), F32),
            pltpu.VMEM((size, size), BF16),
            pltpu.VMEM((size, size), BF16),
            pltpu.VMEM((size, size), BF16),
        ],
        compiler_params=pltpu.CompilerParams(vmem_limit_bytes=24 << 20),
        cost_estimate=pl.CostEstimate(flops=12 * size**3, bytes_accessed=8 * size**2, transcendentals=0),
        name="inverse",
    )(*own, *other)


def rows_kernel(counts, *refs):
    *h_refs, v_hi_ref, v_lo_ref, scale_ref, out_ref = refs
    width = out_ref.shape[1]
    parts = []
    for count in counts:
        addends, h_refs = h_refs[:count], h_refs[count:]
        total = addends[0][:, :width]
        for ref in addends[1:]:
            total = total + ref[:, :width]
        parts.append(total)
    h = jnp.concatenate(parts, axis=0)
    hi = h.astype(BF16)
    lo = (h - hi.astype(F32)).astype(BF16)
    times = functools.partial(jnp.dot, preferred_element_type=F32)
    product = times(v_hi_ref[...], hi) + times(v_hi_ref[...], lo) + times(v_lo_ref[...], hi)
    out_ref[...] = (scale_ref[0:1, 0:1] * (2.0**ITERS * h - product)).astype(BF16)


def solve_rows(parts, v_hi, v_lo, scale):
    width = parts[0][-1].shape[1]
    flat = [x for part in parts for x in part]
    return pl.pallas_call(
        functools.partial(rows_kernel, tuple(len(part) for part in parts)),
        out_shape=jax.ShapeDtypeStruct((v_hi.shape[0], width), BF16),
        in_specs=[pl.BlockSpec(memory_space=pltpu.VMEM)] * (len(flat) + 3),
        out_specs=pl.BlockSpec(memory_space=pltpu.VMEM),
        compiler_params=pltpu.CompilerParams(vmem_limit_bytes=24 << 20),
        cost_estimate=pl.CostEstimate(flops=6 * width * B * B, bytes_accessed=4 * B * B, transcendentals=0),
        name="solve_rows",
    )(*flat, v_hi, v_lo, scale)


def pruned_kernel(weight_ref, mask_ref, out_ref):
    out_ref[...] = jnp.where(mask_ref[...] == 0, weight_ref[...], jnp.zeros((), BF16))


def narrow_kernel(mask_ref, out_ref):
    out_ref[...] = mask_ref[...].astype(F32).astype(BF16)


def pruned_columns(weight, mask, width):
    if width % 128:
        return jnp.where(mask[:, :width] == 0, weight[:, :width], jnp.zeros((), BF16))
    block = pl.BlockSpec((weight.shape[0], width), lambda i: (0, 0))
    return pl.pallas_call(
        pruned_kernel,
        out_shape=jax.ShapeDtypeStruct((weight.shape[0], width), BF16),
        grid=(1,),
        in_specs=[block, block],
        out_specs=block,
        compiler_params=pltpu.CompilerParams(vmem_limit_bytes=8 << 20),
        cost_estimate=pl.CostEstimate(flops=0, bytes_accessed=8 * weight.shape[0] * width, transcendentals=0),
        name="pruned_columns",
    )(weight, mask)


def narrowed(mask):
    rows, columns = mask.shape
    block = pl.BlockSpec((min(512, rows), columns), lambda i: (i, 0))
    return pl.pallas_call(
        narrow_kernel,
        out_shape=jax.ShapeDtypeStruct(mask.shape, BF16),
        grid=(rows // min(512, rows),),
        in_specs=[block],
        out_specs=block,
        compiler_params=pltpu.CompilerParams(vmem_limit_bytes=12 << 20),
        cost_estimate=pl.CostEstimate(flops=0, bytes_accessed=6 * mask.size, transcendentals=0),
        name="narrowed",
    )(mask)


def update_kernel(runs, counts, index_ref, weight_ref, mask_ref, pruned_ref, *rest):
    out_ref, stage, sems = rest[-3:]
    pieces = []
    for count in counts:
        pieces.append(rest[:count])
        rest = rest[count:]
    rows = weight_ref.shape[0]
    _, tile, width = stage.shape
    copies = []
    for i in range(0, rows, tile):
        for m, piece in zip(runs, pieces):
            slot = len(copies)
            place = (slice(i, i + tile), pl.ds(pl.multiple_of((index_ref[0] ^ m) * width, width), width))
            fix, start = 0.0, 0
            for part in piece:
                left = pruned_ref[i : i + tile, start : start + part.shape[0]]
                fix += jnp.dot(left, part[...], preferred_element_type=F32)
                start += part.shape[0]
            kept = weight_ref[place].astype(F32) - fix
            stage[slot] = (mask_ref[place].astype(F32) * kept).astype(BF16)
            copy = pltpu.make_async_copy(stage.at[slot], out_ref.at[place], sems.at[slot])
            copy.start()
            copies.append(copy)
    for copy in copies:
        copy.wait()


def update(weight, mask, pruned, pieces, runs, result=None):
    rows, columns = weight.shape
    width = pieces[0][0].shape[1]
    counts = tuple(len(piece) for piece in pieces)
    pieces = [part for piece in pieces for part in piece]
    tile = min(512, rows)
    index = lax.axis_index("tok").astype(jnp.int32).reshape(1)
    extra = [] if result is None else [result]
    count = rows // tile * len(runs)
    return pl.pallas_call(
        functools.partial(update_kernel, runs, counts),
        out_shape=jax.ShapeDtypeStruct((rows, columns), BF16),
        in_specs=[pl.BlockSpec(memory_space=pltpu.SMEM)]
        + [pl.BlockSpec(memory_space=pltpu.VMEM)] * (3 + len(pieces))
        + [pl.BlockSpec(memory_space=pl.ANY)] * len(extra),
        out_specs=pl.BlockSpec(memory_space=pl.ANY),
        scratch_shapes=[pltpu.VMEM((count, tile, width), BF16), pltpu.SemaphoreType.DMA((count,))],
        input_output_aliases={4 + len(pieces): 0} if extra else {},
        compiler_params=pltpu.CompilerParams(vmem_limit_bytes=20 << 20),
        cost_estimate=pl.CostEstimate(
            flops=2 * rows * width * len(runs) * B,
            bytes_accessed=6 * rows * width * len(runs),
            transcendentals=0,
        ),
        name="update",
    )(index, weight, mask, pruned, *pieces, *extra)


def updated(weight, mask, pruned, pieces):
    width = pieces[0][0].shape[1]
    if width % 128:
        order = jnp.arange(len(pieces), dtype=jnp.int32) ^ lax.axis_index("tok")
        whole = [jnp.concatenate(piece, axis=0) for piece in pieces]
        whole = jnp.take(jnp.stack(whole, axis=1), order, axis=1).reshape(B, -1)
        fix = jnp.dot(pruned, whole, preferred_element_type=F32)
        return (mask.astype(F32) * (weight.astype(F32) - fix)).astype(BF16)
    *most, last = pieces
    result = update(weight, mask, pruned, most, tuple(range(len(most))))
    return update(weight, mask, pruned, [last], (len(most),), result)


def gather_and_sum(activations, n_col, n_tok, bits, turned):
    chips = n_col // 2
    own = activations[:, : B // n_col]
    panels, sums, parts = [], [], []
    for k in range(chips):
        mine = own if k == 0 else shift_chip(own, n_col, k)
        panels += [mine, swap_core(mine, n_col)]
        order = turned if k % 2 else bits
        if k:
            rows = (0, 1) if k == 1 else (k,)
            sums.append(sum_tok(block_rows(panels, rows), n_tok, order))
        products = panel_products(panels[-2:], activations, halving(order))
        parts.append(scatter_tok(*products, n_tok, order))
    return sums, [swap_core(x, n_col) for x in sums], parts, mine


def gather_and_sum_4(activations, n_col, n_tok, bits, turned):
    x, y = bits
    own = activations[:, : B // n_col]

    def swapped(array):
        return swap_core(array, n_col)

    def over(array, bit):
        return swap_tok(array, n_tok, bit)

    def added(a, b):
        return add_rounded(a, b)

    def second_step(kept, arrived, bit):
        width = kept.shape[1] // 2
        total = kept[:, width:] + arrived[:, width:]
        return [kept, arrived, over(total, bit)]

    first = shift_chip(own, n_col, 1)
    second = shift_chip(own, n_col, -1)
    third = shift_chip(first, n_col, 1)
    panels = [own, swapped(own)]
    sent, kept = panel_products(panels[:1], activations, halving(bits))
    part_0 = second_step(kept, over(sent, x), y)
    sent, kept = panel_products(panels[1:], activations, halving(turned))
    part_0b = second_step(kept, over(sent, y), x)

    panels += [first, swapped(first)]
    rows_1 = block_rows(panels, (0, 1))
    total_1 = added(rows_1, over(rows_1, x))
    sum_1 = added(total_1, over(total_1, y))
    sent, kept = panel_products(panels[2:3], activations, halving(bits))
    part_1 = second_step(kept, over(sent, x), y)
    sent, kept = panel_products(panels[3:], activations, halving(turned))
    part_2 = second_step(kept, over(sent, y), x)

    panels += [second, swapped(second)]
    rows_2 = block_rows(panels, (2,))
    middle = rows_2.shape[1] // 2
    left, right = rows_2[:, :middle], rows_2[:, middle:]
    left = added(left, over(left, x))
    right = added(right, over(right, y))
    left = added(left, over(left, y))
    right = added(right, over(right, x))
    sum_2 = jnp.concatenate([left, right], axis=1)
    sent, kept = panel_products(panels[4:5], activations, halving(bits))
    part_3 = second_step(kept, over(sent, x), y)
    sent, kept = panel_products(panels[5:], activations, halving(turned))
    part_4 = second_step(kept, over(sent, y), x)

    panels += [third, swapped(third)]
    width = 2 * own.shape[1]
    behind = shift_chip(sum_2, n_col, -1)
    before = shift_chip(sum_1[:, width : 2 * width], n_col, 1)
    sum_3 = [behind[:, width : 2 * width], before, behind[:, :width], behind[:, 2 * width :]]
    sum_3 = jnp.concatenate(sum_3, axis=1)
    products = panel_products(panels[6:], activations, ((0,), (1,), (2,), (3,)))
    part_5 = [products[0]] + [over(products[m], m) for m in (x, y, x | y)]

    sums = [sum_1, sum_2, sum_3]
    others = [swapped(v) for v in sums]
    return sums, others, [part_0, part_0b, part_1, part_2, part_3, part_4, part_5], sum_3


def per_device(activations, weight, keep_mask):
    n_col = lax.axis_size("col")
    n_tok = lax.axis_size("tok")
    panel_width = B // n_col
    chips = n_col // 2
    bits = [1 << k for k in range(n_tok.bit_length() - 1)]
    turned = bits[len(bits) // 2 :] + bits[: len(bits) // 2]

    gather = gather_and_sum_4 if (chips, n_tok) == (4, 4) else gather_and_sum
    sums, others, parts, _ = gather(activations, n_col, n_tok, bits, turned)
    v_hi, v_lo, scale = inverse(sums, others)
    solved = solve_rows(parts, v_hi, v_lo, scale)
    pieces = gather_tok(solved, n_tok)

    mask = narrowed(keep_mask)
    pruned = pruned_columns(weight, mask, panel_width)
    if chips == 4:
        second = shift_chip(pruned, n_col, 1)
        third = shift_chip(second, n_col, 1)
        half = pruned.shape[0] // 2
        fourth = [shift_chip(pruned[:half], n_col, -1), shift_chip(pruned[half:], n_col, -1)]
        pruned = [pruned, second, jnp.concatenate(fourth, axis=0), third]
    else:
        pruned = [pruned] + [shift_chip(pruned, n_col, k) for k in range(1, chips)]
    others = [swap_core(v, n_col) for v in pruned]
    pruned_panel = jnp.concatenate([x for pair in zip(pruned, others) for x in pair], axis=1)
    return updated(weight, mask, pruned_panel, pieces)


def solution(mesh):
    return jax.shard_map(
        per_device,
        mesh=mesh,
        in_specs=(P("tok", "col"), P("tok", "col"), P("tok", "col")),
        out_specs=P("tok", "col"),
        check_vma=False,
    )
```
